256 devices in a mesh: dp: 8 (over y, x_lo), feat: 32 (over x_hi, z, core).
Axes of the slice: x: 4 (x_hi: 2, x_lo: 2; x = x_hi * 2 + x_lo), y: 4, z: 8, core: 2. Of those that a mesh axis runs over, the one named last changes fastest.
Arguments:
- features: bfloat16 [4096, 16384], P('dp', 'feat'), may hold values from -6 to 6
- weight: bfloat16 [64, 7, 256, 1024], P('feat', None, None, 'dp'), may hold values from -0.125 to 0.125
- cotangent: bfloat16 [4096, 65536], P('dp', 'feat'), may hold values from -6 to 6
Outputs:
- activated: bfloat16 [4096, 65536], P('dp', 'feat')
- grad_input: bfloat16 [4096, 16384], P('dp', 'feat')
- grad_weight: float32 [64, 7, 256, 1024], P('feat', None, None, 'dp')
The draws below stay inside these ranges and needn't reach their ends.
All inputs are finite; a program needn't handle non-finite values.
Results may differ from the reference program's by a relative error of at most 0.0049.
Values may be sent and summed in bfloat16 or wider, within the bound.
No kernel may reach another device: no remote copies, remote signals or barrier semaphores. Data moves between devices by JAX's collectives and lax.ppermute only.
A program may use at most 128 MiB of HBM per device.

```python
import jax
import jax.numpy as jnp
from jax import lax

D = 16384
FF = 65536
BLK = 256
TAPS = 7
TOKENS = 4096
NB = 64
GROUP_COLS = 1024


def block_scale(own_key, extent, split, smallest, high):
    level = 1.0
    for dim, shards_of in split:
        draws = jax.random.uniform(jax.random.fold_in(jax.random.fold_in(own_key, 6), dim), (shards_of,), jnp.float32, smallest / len(split), high / len(split))
        level = level * jnp.repeat(jnp.exp(draws), extent[dim] // shards_of).reshape((-1,) + (1,) * (len(extent) - 1 - dim))
    return level


def noise(own_key, extent, scale, limit, pieces=(), kind=jnp.bfloat16):
    factor_of = block_scale(own_key, extent, pieces, -0.22, 0.18) if pieces else 1.0
    result = jax.random.normal(own_key, extent, jnp.float32) * scale * factor_of
    return jnp.minimum(jnp.maximum(result, -limit), limit).astype(kind)


def setup_inputs(seed: int = 0) -> dict:
    keys = jax.random.split(jax.random.key(seed), 4)
    return {
        "features": noise(keys[0], (TOKENS, D), 1.0, 6.0, ((0, 8), (1, 32))),
        "weight": noise(keys[1], (NB, TAPS, BLK, GROUP_COLS), (TAPS * BLK) ** -0.5, 0.125, ((0, 32), (3, 8))),
        "cotangent": noise(keys[2], (TOKENS, FF), 1.0, 6.0, ((0, 8), (1, 32))),
    }


gelu_scale = 0.7978845608
gelu_cubic = 0.044715

def gelu(values):
    return 0.5 * values * (1.0 + jnp.tanh(gelu_scale * (values + gelu_cubic * values * values * values)))

def reference(features, weight, cotangent):
    in_count = D // BLK
    group_cols = FF // in_count
    distances = jnp.array([0] + [2 ** k for k in range(TAPS - 1)], jnp.int32)
    in_blocks = features.reshape(TOKENS, in_count, BLK)
    out_grads = cotangent.reshape(TOKENS, in_count, group_cols)
    factor = float(TOKENS) ** (-0.5)

    def group_step(running, group):
        sources = jnp.bitwise_xor(group, distances).astype(jnp.int32)
        tap_rows = jnp.take(in_blocks, sources, axis=1).astype(jnp.float32)
        group_weight = lax.dynamic_index_in_dim(weight, group, 0, keepdims=False).astype(jnp.float32)
        before = jnp.einsum('ntb,tbc->nc', tap_rows, group_weight)
        after = gelu(before).astype(jnp.bfloat16)
        _, backward = jax.vjp(gelu, before)
        given = lax.dynamic_index_in_dim(out_grads, group, 1, keepdims=False).astype(jnp.float32)
        grad_pre = backward(given)[0].astype(jnp.bfloat16).astype(jnp.float32)
        partial_value = jnp.einsum('nc,tbc->ntb', grad_pre, group_weight)
        running = running.at[:, sources].add(partial_value)
        grad_group = jnp.einsum('ntb,nc->tbc', tap_rows, grad_pre) * factor
        return (running, (after, grad_group))
    start = jnp.zeros((TOKENS, in_count, BLK), jnp.float32)
    grad_blocks, (outputs, grad_weight) = lax.scan(group_step, start, jnp.arange(in_count, dtype=jnp.int32))
    activated = outputs.transpose(1, 0, 2).reshape(TOKENS, FF)
    grad_input = grad_blocks.reshape(TOKENS, D).astype(jnp.bfloat16)
    return (activated, grad_input, grad_weight)
```

```python
import jax
import jax.numpy as jnp
from jax import lax
from jax.sharding import Mesh
from jax.sharding import PartitionSpec as P


gelu_scale = 0.7978845608
gelu_cubic = 0.044715
bf16 = jnp.bfloat16
f32 = jnp.float32


def flip(array, axis, bit):
    return lax.ppermute(array, axis, [(i, i ^ 1 << bit) for i in range(lax.axis_size(axis))])


def shift(array, axis, step):
    n = lax.axis_size(axis)
    return lax.ppermute(array, axis, [(i, (i + step) % n) for i in range(n)])


def gelu(values):
    return (
        0.5
        * values
        * (1.0 + jnp.tanh(gelu_scale * (values + gelu_cubic * values * values * values)))
    )


def gather_shards(shard, a_rows):
    rows = shard.shape[0]
    half, a_half = rows // 2, a_rows // 2
    up = shift(shard, "y", 1)
    down = shift(shard, "y", -1)
    side = flip(shard, "xl", 0)
    a = side[:a_rows]
    side_up = shift(a, "y", 1)
    side_down = shift(a, "y", -1)
    far_lo = shift(up[:half], "y", 1)
    far_hi = shift(down[half:], "y", -1)
    up_b = flip(up[a_rows:], "xl", 0)
    down_b = flip(down[a_rows:], "xl", 0)
    sfar_lo = shift(side_up[:a_half], "y", 1)
    sfar_hi = shift(side_down[a_half:], "y", -1)
    far_b = flip(far_hi[a_rows - half:], "xl", 0)
    return {
        (0, 0): [shard],
        (3, 0): [up],
        (1, 0): [down],
        (2, 0): [far_lo, far_hi],
        (0, 1): [side],
        (3, 1): [side_up, up_b],
        (1, 1): [side_down, down_b],
        (2, 1): [sfar_lo, sfar_hi, far_b],
    }


def reduce_shards(part, a_rows):
    rows = part[0, 0].shape[0]
    half, a_half = rows // 2, a_rows // 2

    def add(x, *more):
        total = x.astype(f32)
        for m in more:
            total = total + m.astype(f32)
        return total.astype(bf16)

    far_s = part[2, 1]
    s_lo = shift(far_s[:a_half], "y", -1)
    s_hi = shift(far_s[a_half:a_rows], "y", 1)
    far_b = flip(far_s[a_rows:], "xl", 0)
    m_up = part[3, 1]
    m_down = part[1, 1]
    u = jnp.concatenate([add(m_up[:a_half], s_lo), m_up[a_half:a_rows]])
    d = jnp.concatenate([m_down[:a_half], add(m_down[a_half:a_rows], s_hi)])
    u_in = shift(u, "y", -1)
    d_in = shift(d, "y", 1)
    far = part[2, 0]
    f_lo = shift(far[:half], "y", -1)
    f_hi = shift(jnp.concatenate([far[half:a_rows], add(far[a_rows:], far_b)]), "y", 1)
    up_b = flip(m_up[a_rows:], "xl", 0)
    down_b = flip(m_down[a_rows:], "xl", 0)
    n_up, n_down = part[3, 0], part[1, 0]
    nu = jnp.concatenate([add(n_up[:half], f_lo), n_up[half:a_rows], add(n_up[a_rows:], up_b)])
    nd = jnp.concatenate([n_down[:half], add(n_down[half:a_rows], f_hi[:a_rows - half]),
                          add(n_down[a_rows:], f_hi[a_rows - half:], down_b)])
    sd = part[0, 1]
    sd = jnp.concatenate([add(sd[:a_rows], u_in, d_in), sd[a_rows:]])
    r1 = shift(nu, "y", -1)
    r2 = shift(nd, "y", 1)
    r3 = flip(sd, "xl", 0)
    return part[0, 0].astype(f32) + r1.astype(f32) + r2.astype(f32) + r3.astype(f32)


def on_device(features, weight, cotangent):
    n = features.shape[0]
    groups, taps, blk, cols = weight.shape
    x = features.reshape(n, groups, blk)
    tiles = groups * taps
    a_rows = (tiles * 5 // 7) * blk
    got = gather_shards(weight.reshape(tiles * blk, cols), a_rows)
    partners = [
        flip(features, "z", 2),
        flip(features, "z", 1),
        flip(features, "z", 0),
        flip(features, "xh", 0),
        flip(features, "c", 0),
    ]
    z4, z2, z1, xh, c1 = partners
    tap_in = [x, x[:, ::-1]] + [p.reshape(n, groups, blk) for p in (c1, z1, z2, z4, xh)]
    stacked = jnp.stack(tap_in, axis=1)
    y, xl = lax.axis_index("y"), lax.axis_index("xl")

    rel = [(dy, dx) for dy in range(4) for dx in range(2)]
    whole = [jnp.concatenate(got[k]).reshape(groups, taps, blk, cols) for k in rel]
    w = jnp.concatenate(whole, axis=3)
    cot = cotangent.reshape(n, groups, 4, 2, cols)

    def to_rel(a):
        a = jnp.where(xl == 1, a[..., ::-1, :], a)
        return jnp.roll(a, -y, axis=-3)

    def to_abs(a):
        a = jnp.roll(a, y, axis=-3)
        return jnp.where(xl == 1, a[..., ::-1, :], a)

    cot = to_rel(cot).reshape(n, groups, 8 * cols)
    before = jnp.einsum("ntgb,gtbc->ngc", stacked, w, preferred_element_type=f32)
    activated = to_abs(gelu(before).astype(bf16).reshape(n, groups, 4, 2, cols)).reshape(n, -1)
    _, backward = jax.vjp(gelu, before)
    grad_pre = backward(cot.astype(f32))[0].astype(bf16)
    term = jnp.einsum("ntgb,ngc->gtbc", stacked, grad_pre, preferred_element_type=f32).astype(bf16)
    part = {k: term[..., i * cols:(i + 1) * cols].reshape(tiles * blk, cols) for i, k in enumerate(rel)}
    gw = reduce_shards(part, a_rows)
    partial = jnp.einsum("ngc,gtbc->ntgb", grad_pre, w, preferred_element_type=f32)
    sends = [partial[:, t].astype(bf16).reshape(n, -1) for t in (5, 4, 3, 6, 2)]
    back = [flip(sends[0], "z", 2), flip(sends[1], "z", 1), flip(sends[2], "z", 0),
            flip(sends[3], "xh", 0), flip(sends[4], "c", 0)]
    total = (partial[:, 0] + partial[:, 1, ::-1]).reshape(n, -1)
    for b in back:
        total = total + b.astype(f32)
    factor = float(n * 8) ** (-0.5)
    return (activated, total.astype(bf16), gw.reshape(weight.shape) * factor)


def solution(mesh):
    torus = Mesh(mesh.devices.reshape(4, 2, 2, 8, 2), ("y", "xl", "xh", "z", "c"))
    dp, feat = ("y", "xl"), ("xh", "z", "c")
    placed = (P(dp, feat), P(feat, None, None, dp), P(dp, feat))
    return jax.shard_map(
        on_device,
        mesh=torus,
        in_specs=placed,
        out_specs=(P(dp, feat), P(dp, feat), P(feat, None, None, dp)),
        check_vma=False,
    )
```

```python
import functools

import jax
import jax.numpy as jnp
from jax import lax
from jax.experimental import pallas as pl
from jax.experimental.pallas import tpu as pltpu
from jax.sharding import Mesh
from jax.sharding import PartitionSpec as P


gelu_scale = 0.7978845608
gelu_cubic = 0.044715
bf16 = jnp.bfloat16
f32 = jnp.float32
MIB = 1024 * 1024


def flip(array, axis, mask):
    return lax.ppermute(array, axis, [(i, i ^ mask) for i in range(lax.axis_size(axis))])


def shift(array, axis, step):
    n = lax.axis_size(axis)
    return lax.ppermute(array, axis, [(i, (i + step) % n) for i in range(n)])


def up(a):
    return shift(a, "y", 1)


def down(a):
    return shift(a, "y", -1)


def side(a):
    return flip(a, "xl", 1)


class Dims:
    def __init__(self, features, weight):
        self.n = features.shape[0]
        self.groups, self.taps, self.blk, self.cols = weight.shape
        self.tiles = self.groups * self.taps
        self.width = self.groups * 8 * self.cols


def vspec():
    return pl.BlockSpec(memory_space=pltpu.VMEM)


def call(body, operands, shapes, limit, flops=0, moved=0, specs=None, out_specs=None,
         scratch=(), aliases=None):
    return pl.pallas_call(
        body,
        out_shape=shapes,
        in_specs=specs or [vspec()] * len(operands),
        out_specs=out_specs or [vspec()] * len(shapes),
        scratch_shapes=scratch,
        input_output_aliases=aliases or {},
        compiler_params=pltpu.CompilerParams(vmem_limit_bytes=limit * MIB),
        cost_estimate=pl.CostEstimate(flops=flops, bytes_accessed=moved, transcendentals=0),
    )(*operands)


class Tiles:
    def __init__(self, *parts):
        self.where = {}
        for array, row, tiles in parts:
            for i, tile in enumerate(tiles):
                self.where[tile] = (array, row + i)


class Operands:
    def __init__(self):
        self.arrays = []

    def add(self, array):
        for i, a in enumerate(self.arrays):
            if a is array:
                return i
        self.arrays.append(array)
        return len(self.arrays) - 1

    def shard(self, tiles, d, group=None):
        return {t: (self.add(a), r) for t, (a, r) in tiles.where.items()
                if group is None or t // d.taps == group}


def tile_of(d, refs, shard, g, t):
    ref, row = shard[g * d.taps + t]
    return refs[ref][row * d.blk:(row + 1) * d.blk, :]


def source(g, t):
    return (0, g ^ t) if t < 2 else (t - 1, g)


def forward_body(d, steps, shards, count, xs, has_act, rolled, *refs):
    ops, rest = refs[:count], list(refs[count:])
    cot = ops[0]
    if has_act:
        rest.pop(0)
    act, gps, buf, sem = rest
    y, xl = lax.axis_index("y"), lax.axis_index("xl")
    half = d.n // 2
    two = 2 * d.cols
    copies = []
    for i, (dy, g) in enumerate(steps):
        base = ((y + dy) & 3) * two + g * (8 * d.cols)
        cols = [pl.multiple_of(base + (xl ^ dx) * d.cols, d.cols) for dx in range(2)]
        w = jnp.concatenate(
            [jnp.concatenate([tile_of(d, ops, shards[dy, dx], g, t) for dx in range(2)], axis=1)
             for t in range(d.taps)], axis=0)

        def rows_step(rows):
            x = []
            for t in range(d.taps):
                ref, blk = xs[source(g, t)]
                x.append(ops[ref][rows, blk * d.blk:(blk + 1) * d.blk])
            v = jnp.dot(jnp.concatenate(x, axis=1), w, preferred_element_type=f32)
            for dx in range(2):
                vv = v[:, dx * d.cols:(dx + 1) * d.cols]
                c = cot[rows, pl.ds(cols[dx], d.cols)].astype(f32)
                sq = vv * vv
                t = jnp.tanh(vv * (gelu_scale + (gelu_scale * gelu_cubic) * sq))
                h = 0.5 + 0.5 * t
                a = vv * h
                buf[i, dx, rows, :] = a.astype(bf16)
                slope = gelu_scale + (3.0 * gelu_scale * gelu_cubic) * sq
                grad = c * (h + a * (1.0 - t) * slope)
                gps[i, rows, dx * d.cols:(dx + 1) * d.cols] = grad.astype(bf16)

        if rolled:
            pl.loop(0, 2)(lambda r: rows_step(pl.ds(pl.multiple_of(r * half, half), half)))
        else:
            for r in range(2):
                rows_step(slice(r * half, (r + 1) * half))
        for dx in range(2):
            copy = pltpu.make_async_copy(
                buf.at[i, dx], act.at[:, pl.ds(cols[dx], d.cols)], sem.at[i, dx])
            copy.start()
            copies.append(copy)
    for copy in copies:
        copy.wait()


def forward(d, steps, xs, cot, ws, act=None, rolled=False):
    slots = len(steps)
    ops = Operands()
    ops.add(cot)
    need = {source(g, t) for _, g in steps for t in range(d.taps)}
    xs = {k: (ops.add(a), blk) for k, (a, blk) in xs.items() if k in need}
    shards = {}
    for dy, g in steps:
        for dx in range(2):
            shards.setdefault((dy, dx), {}).update(ops.shard(ws[dy, dx], d, g))
    operands = list(ops.arrays)
    count = len(operands)
    specs = [vspec()] * count
    aliases = {}
    if act is not None:
        aliases = {count: 0}
        operands.append(act)
        specs.append(pl.BlockSpec(memory_space=pl.ANY))
    out = call(
        functools.partial(forward_body, d, steps, shards, count, xs, act is not None, rolled),
        operands,
        [jax.ShapeDtypeStruct((d.n, d.width), bf16),
         jax.ShapeDtypeStruct((slots, d.n, 2 * d.cols), bf16)],
        22, 2 * d.n * d.taps * d.blk * 2 * d.cols * slots, 8 * d.n * d.cols * slots,
        specs=specs, out_specs=[pl.BlockSpec(memory_space=pl.ANY), vspec()],
        scratch=[pltpu.VMEM((slots, 2, d.n, d.cols), bf16), pltpu.SemaphoreType.DMA((slots, 2))],
        aliases=aliases)
    return out[0], {step: (out[1], i) for i, step in enumerate(steps)}


def wgrad_body(d, steps, where, count, xts, gps, copied, *refs):
    ops, outs = refs[:count], refs[count:]
    part = d.blk // 2
    for out, row, ref, rows in copied:
        outs[out][row * d.blk:(row + rows) * d.blk, :] = ops[ref][...]
    for dy, g in steps:
        ref, at = gps[dy, g]
        gp = ops[ref][at]

        @pl.loop(0, 2)
        def _(r):
            for t in range(d.taps):
                ref, blk = xts[source(g, t)]
                rows = pl.ds(pl.multiple_of(blk * d.blk + r * part, part), part)
                v = jnp.dot(ops[ref][rows, :], gp, preferred_element_type=f32)
                for dx in range(2):
                    out, row = where[dy, dx][g * d.taps + t]
                    rows = pl.ds(pl.multiple_of(row * d.blk + r * part, part), part)
                    outs[out][rows, :] = v[:, dx * d.cols:(dx + 1) * d.cols].astype(outs[out].dtype)


def wgrad(d, steps, xts, gps, pieces, carried=None):
    ops = Operands()
    where = {(dy, dx): {} for dy, _ in steps for dx in range(2)}
    shapes, copied = [], []
    for i, piece in enumerate(pieces):
        row = 0
        if carried and i in carried:
            row = carried[i].shape[0] // d.blk
            copied.append((i, 0, ops.add(carried[i]), row))
        for owner, tiles in piece:
            for tile in tiles:
                where[owner][tile] = (i, row)
                row += 1
        kind = f32 if owner == (0, 0) else bf16
        shapes.append(jax.ShapeDtypeStruct((row * d.blk, d.cols), kind))
    need = {source(g, t) for _, g in steps for t in range(d.taps)}
    xts = {k: (ops.add(a), blk) for k, (a, blk) in xts.items() if k in need}
    gps = {step: (ops.add(gps[step][0]), gps[step][1]) for step in steps}
    count = len(ops.arrays)
    return call(functools.partial(wgrad_body, d, steps, where, count, xts, gps, copied),
                ops.arrays, shapes, 20,
                4 * d.n * d.taps * d.blk * d.cols * len(steps), 2 * d.n * d.n * len(steps))


def dgrad_body(d, outs_of, shards, count, gps, *refs):
    ops, outs = refs[:count], refs[count:]
    half = d.n // 2
    for out, jobs in zip(outs, outs_of):
        for lane, products in enumerate(jobs):
            w = jnp.concatenate([tile_of(d, ops, shards[dy, dx], g, t) for t, g in products
                                 for dy in range(4) for dx in range(2)], axis=1)
            for r in range(2):
                rows = slice(r * half, (r + 1) * half)
                gp = jnp.concatenate([ops[gps[dy, g][0]][gps[dy, g][1], rows, :]
                                      for _, g in products for dy in range(4)], axis=1)
                v = lax.dot_general(gp, w, (((1,), (1,)), ((), ())), preferred_element_type=f32)
                out[rows, lane * d.blk:(lane + 1) * d.blk] = v.astype(out.dtype)


def dgrad(d, outs, gps, ws):
    ops = Operands()
    groups = sorted({g for o in outs for job in o for _, g in job})
    gps = {(dy, g): (ops.add(gps[dy, g][0]), gps[dy, g][1]) for dy in range(4) for g in groups}
    shards = {o: {} for o in ws}
    for o in ws:
        for g in groups:
            shards[o].update(ops.shard(ws[o], d, g))
    count = len(ops.arrays)
    jobs = sum(len(j) for o in outs for j in o)
    shapes = [jax.ShapeDtypeStruct((d.n, d.blk * len(o)), f32 if len(o[0]) > 1 else bf16)
              for o in outs]
    return call(functools.partial(dgrad_body, d, outs, shards, count, gps), ops.arrays, shapes,
                20, 16 * d.n * jobs * d.blk * d.cols, d.n * d.n * jobs)


def transpose_body(*refs):
    k = len(refs) // 2
    for a, b in zip(refs[:k], refs[k:]):
        b[...] = a[...].T


def transposed(xs):
    return call(transpose_body, xs,
                [jax.ShapeDtypeStruct(x.shape[::-1], x.dtype) for x in xs], 12, 0, 1 << 20)


def combine_body(plan, count, scale, *refs):
    outs = refs[count:]
    step = 256
    for out, pieces in zip(outs, plan):
        for lo, hi, terms in pieces:
            @pl.loop(0, (hi - lo) // step)
            def _(i):
                total = None
                for ref, row in terms:
                    term = refs[ref][pl.ds(pl.multiple_of(row + i * step, step), step), :]
                    if len(terms) > 1:
                        term = term.astype(f32)
                    total = term if total is None else total + term
                if scale is not None:
                    total = total * scale
                out[pl.ds(pl.multiple_of(lo + i * step, step), step), :] = total.astype(out.dtype)


def combine(outs, dtype=bf16, scale=None):
    ops = Operands()
    plan, shapes = [], []
    for pieces in outs:
        lo, entry = 0, []
        for rows, terms in pieces:
            entry.append((lo, lo + rows, [(ops.add(a), r) for a, r in terms]))
            lo += rows
        plan.append(entry)
        shapes.append(jax.ShapeDtypeStruct((lo, pieces[0][1][0][0].shape[1]), dtype))
    return call(functools.partial(combine_body, plan, len(ops.arrays), scale), ops.arrays,
                shapes, 16, 0, 1 << 20)


def grad_input_body(d, count, *refs):
    whole, halves, out = refs[:count], refs[count:-1], refs[-1]
    per = len(halves) // d.groups
    step = 128

    @pl.loop(0, d.n // step)
    def _(i):
        rows = pl.ds(pl.multiple_of(i * step, step), step)
        for g in range(d.groups):
            lanes = slice(g * d.blk, (g + 1) * d.blk)
            total = whole[0][rows, lanes]
            for ref in whole[1:]:
                total = total + ref[rows, lanes].astype(f32)
            for ref in halves[g * per:(g + 1) * per]:
                total = total + ref[rows, :].astype(f32)
            out[rows, lanes] = total.astype(out.dtype)


def grad_input(d, here, whole, halves):
    return call(functools.partial(grad_input_body, d, 1 + len(whole)),
                [here, *whole, *halves[0], *halves[1]],
                [jax.ShapeDtypeStruct((d.n, d.groups * d.blk), bf16)], 16, 0, 1 << 20)[0]


def step(features, weight, cotangent):
    d = Dims(features, weight)
    w = weight.reshape(d.tiles * d.blk, d.cols)
    t_a, t_l, t_h = range(0, 10), range(0, 5), range(5, 10)
    t_b, t_0, t_1, t_all = range(10, 14), range(0, 7), range(7, 14), range(14)
    h_0, h_1 = range(5, 7), range(7, 10)
    A, L, B, G = 10 * d.blk, 5 * d.blk, 4 * d.blk, 7 * d.blk

    u, m = up(w), down(w)
    wa, wb = combine([[(A, [(w, 0)])], [(B, [(w, A)])]])
    sa = side(wa)
    su, sm = up(sa), down(sa)
    ulo, mhi, ub = combine([[(G, [(u, 0)])], [(G, [(m, G)])],
                            [(B, [(u, A)]), (B, [(m, A)]), (B, [(wb, 0)])]])
    fl, fh, ub = up(ulo), down(mhi), side(ub)
    slo, shi = combine([[(L, [(su, 0)])], [(L, [(sm, L)])]])
    gl, gh = up(slo), down(shi)
    gb = side(combine([[(B, [(fh, A - G)])]])[0])
    ws = {
        (0, 0): Tiles((w, 0, t_all)),
        (3, 0): Tiles((u, 0, t_all)),
        (1, 0): Tiles((m, 0, t_all)),
        (2, 0): Tiles((fl, 0, t_0), (fh, 0, t_1)),
        (0, 1): Tiles((sa, 0, t_a), (ub, 8, t_b)),
        (3, 1): Tiles((su, 0, t_a), (ub, 0, t_b)),
        (1, 1): Tiles((sm, 0, t_a), (ub, 4, t_b)),
        (2, 1): Tiles((gl, 0, t_l), (gh, 0, t_h), (gb, 0, t_b)),
    }

    fa, fb = features[:, :d.blk], features[:, d.blk:]
    x1 = flip(features, "c", 1)
    x2 = [flip(fa, "z", 1), flip(fb, "z", 1)]
    x3 = [flip(fa, "z", 2), flip(fb, "z", 2)]
    x4 = [flip(x3[0], "z", 6), flip(x3[1], "z", 6)]
    x5 = flip(features, "xh", 1)
    keys = [(src, blk) for src in range(6) for blk in range(2)]

    def placed(whole, split):
        it = {0: whole[0], 1: whole[1], 5: whole[2]}
        return {(src, blk): (it[src], blk) if src in it else (split[src - 2][blk], 0)
                for src, blk in keys}

    xs = placed([features, x1, x5], [x2, x3, x4])
    *t_whole, t2a, t3a, t4a = transposed([features, x1, x5, x2[0], x3[0], x4[0]])
    t2b, t3b, t4b = transposed([x2[1], x3[1], x4[1]])
    xts = placed(t_whole, [[t2a, t2b], [t3a, t3b], [t4a, t4b]])

    gps = {}
    act, more = forward(d, [(0, 0)], xs, cotangent, ws, rolled=True)
    gps.update(more)

    def run(steps, rolled=False):
        nonlocal act
        act, more = forward(d, steps, xs, cotangent, ws, act, rolled)
        gps.update(more)

    run([(1, 0), (3, 0)])
    pd, pul, pu0, hu, hd = wgrad(d, [(1, 0), (3, 0)], xts, gps, [
        [((1, 1), t_l), ((1, 0), t_0)], [((3, 1), t_l)], [((3, 0), t_0)],
        [((3, 1), h_0)], [((1, 1), h_0)]])
    r1 = up(pd)
    run([(2, 0)])
    pfl, pf0, hf = wgrad(d, [(2, 0)], xts, gps, [
        [((2, 1), t_l)], [((2, 0), t_0)], [((2, 1), h_0)]])
    el, rfl = down(pfl), down(pf0)
    p5a, p4a = dgrad(d, [[[(5, 0)]], [[(4, 0)]]], gps, ws)
    z5a = flip(p5a, "z", 6)
    p4a, = combine([[(d.n, [(p4a, 0), (z5a, 0)])]])
    z4a = flip(p4a, "z", 2)
    run([(1, 1), (3, 1)])
    puh, pdh, pub, pu1, pd1 = wgrad(d, [(1, 1), (3, 1)], xts, gps, [
        [((3, 1), h_1)], [((1, 1), h_1)], [((3, 1), t_b), ((1, 1), t_b)],
        [((3, 0), t_1)], [((1, 0), t_1)]], {0: hu, 1: hd})
    rub = side(pub)
    run([(2, 1)])
    pfh, pfb, pf1 = wgrad(d, [(2, 1)], xts, gps, [
        [((2, 1), h_1)], [((2, 1), t_b)], [((2, 0), t_1)]], {0: hf})
    eh, eb = up(pfh), side(pfb)
    run([(0, 1)], True)
    p5b, p4b, p3 = dgrad(d, [[[(5, 1)]], [[(4, 1)]], [[(3, 0)], [(3, 1)]]], gps, ws)
    z5b, z3 = flip(p5b, "z", 6), flip(p3, "z", 1)
    p4b, = combine([[(d.n, [(p4b, 0), (z5b, 0)])]])
    z4b = flip(p4b, "z", 2)

    pu, = combine([[(L, [(pul, 0), (el, 0)]), (L, [(puh, 0)])]])
    ru = down(pu)
    rd, = combine([[(L, [(pdh, 0), (eh, 0)]),
                    (A - G, [(pf1, 0)]), (B, [(pf1, A - G), (eb, 0)])]])
    rd = up(rd)
    p6, p2, here = dgrad(d, [
        [[(6, 0)], [(6, 1)]], [[(2, 0)], [(2, 1)]],
        [[(0, 0), (1, 1)], [(0, 1), (1, 0)]]], gps, ws)
    zx, zc = flip(p6, "xh", 1), flip(p2, "c", 1)
    pu, = combine([[(G, [(pu0, 0), (rfl, 0)]), (A - G, [(pu1, 0)]),
                    (B, [(pu1, A - G), (rub, 0)])]])
    q0 = down(pu)
    mine, psa, psb = wgrad(d, [(0, 0), (0, 1)], xts, gps, [
        [((0, 0), t_all)], [((0, 1), t_a)], [((0, 1), t_b)]])
    q2b = side(psb)
    psa, = combine([[(L, [(psa, 0), (ru, 0), (r1, 0)]), (L, [(psa, L), (ru, L), (rd, 0)])]])
    q2a = side(psa)
    pd1, = combine([[(A - G, [(pd1, 0), (rd, L)]),
                     (B, [(pd1, A - G), (rd, L + A - G), (rub, B)])]])
    q1h = up(pd1)
    gx = grad_input(d, here, [zc, z3, zx], [[z4a], [z4b]])
    gw, = combine([[
        (G, [(mine, 0), (q0, 0), (r1, L), (q2a, 0)]),
        (A - G, [(mine, G), (q0, G), (q1h, 0), (q2a, G)]),
        (B, [(mine, A), (q0, A), (q1h, A - G), (q2b, 0)])]],
        f32, float(d.n * 8) ** (-0.5))
    return (act, gx, gw.reshape(weight.shape))


def solution(mesh):
    torus = Mesh(mesh.devices.reshape(4, 2, 2, 8, 2), ("y", "xl", "xh", "z", "c"))
    dp, feat = ("y", "xl"), ("xh", "z", "c")
    placed = (P(dp, feat), P(feat, None, None, dp), P(dp, feat))
    return jax.shard_map(
        step,
        mesh=torus,
        in_specs=placed,
        out_specs=(P(dp, feat), P(dp, feat), P(feat, None, None, dp)),
        check_vma=False,
    )
```

```python
import functools

import jax
import jax.numpy as jnp
from jax import lax
from jax.experimental import pallas as pl
from jax.experimental.pallas import tpu as pltpu
from jax.sharding import Mesh
from jax.sharding import PartitionSpec as P


gelu_scale = 0.7978845608
gelu_cubic = 0.044715
bf16 = jnp.bfloat16
f32 = jnp.float32
MIB = 1024 * 1024


def flip(array, axis, mask):
    return lax.ppermute(array, axis, [(i, i ^ mask) for i in range(lax.axis_size(axis))])


def shift(array, axis, step):
    n = lax.axis_size(axis)
    return lax.ppermute(array, axis, [(i, (i + step) % n) for i in range(n)])


def up(a):
    return shift(a, "y", 1)


def down(a):
    return shift(a, "y", -1)


def side(a):
    return flip(a, "xl", 1)


class Dims:
    def __init__(self, features, weight):
        self.n = features.shape[0]
        self.groups, self.taps, self.blk, self.cols = weight.shape
        self.tiles = self.groups * self.taps
        self.width = self.groups * 8 * self.cols


def vspec():
    return pl.BlockSpec(memory_space=pltpu.VMEM)


def call(body, operands, shapes, limit, flops=0, moved=0, specs=None, out_specs=None,
         scratch=(), aliases=None):
    return pl.pallas_call(
        body,
        out_shape=shapes,
        in_specs=specs or [vspec()] * len(operands),
        out_specs=out_specs or [vspec()] * len(shapes),
        scratch_shapes=scratch,
        input_output_aliases=aliases or {},
        compiler_params=pltpu.CompilerParams(vmem_limit_bytes=limit * MIB),
        cost_estimate=pl.CostEstimate(flops=flops, bytes_accessed=moved, transcendentals=0),
    )(*operands)


class Tiles:
    def __init__(self, *parts):
        self.where = {}
        for array, row, tiles in parts:
            for i, tile in enumerate(tiles):
                self.where[tile] = (array, row + i)


class Operands:
    def __init__(self):
        self.arrays = []

    def add(self, array):
        for i, a in enumerate(self.arrays):
            if a is array:
                return i
        self.arrays.append(array)
        return len(self.arrays) - 1

    def shard(self, tiles, d, group=None):
        return {t: (self.add(a), r) for t, (a, r) in tiles.where.items()
                if group is None or t // d.taps == group}


def tile_of(d, refs, shard, g, t):
    ref, row = shard[g * d.taps + t]
    return refs[ref][row * d.blk:(row + 1) * d.blk, :]


def source(g, t):
    return (0, g ^ t) if t < 2 else (t - 1, g)


def forward_body(d, steps, shards, count, xs, has_act, rolled, *refs):
    ops, rest = refs[:count], list(refs[count:])
    cot = ops[0]
    if has_act:
        rest.pop(0)
    act, gps, buf, sem = rest
    y, xl = lax.axis_index("y"), lax.axis_index("xl")
    half = d.n // 2
    two = 2 * d.cols
    copies = []
    for i, (dy, g) in enumerate(steps):
        base = ((y + dy) & 3) * two + g * (8 * d.cols)
        cols = [pl.multiple_of(base + (xl ^ dx) * d.cols, d.cols) for dx in range(2)]
        w = jnp.concatenate(
            [jnp.concatenate([tile_of(d, ops, shards[dy, dx], g, t) for dx in range(2)], axis=1)
             for t in range(d.taps)], axis=0)

        def rows_step(rows):
            x = []
            for t in range(d.taps):
                ref, blk = xs[source(g, t)]
                x.append(ops[ref][rows, blk * d.blk:(blk + 1) * d.blk])
            v = jnp.dot(jnp.concatenate(x, axis=1), w, preferred_element_type=f32)
            for dx in range(2):
                vv = v[:, dx * d.cols:(dx + 1) * d.cols]
                c = cot[rows, pl.ds(cols[dx], d.cols)].astype(f32)
                sq = vv * vv
                t = jnp.tanh(vv * (gelu_scale + (gelu_scale * gelu_cubic) * sq))
                h = 0.5 + 0.5 * t
                a = vv * h
                buf[i, dx, rows, :] = a.astype(bf16)
                slope = gelu_scale + (3.0 * gelu_scale * gelu_cubic) * sq
                grad = c * (h + a * (1.0 - t) * slope)
                gps[i, rows, dx * d.cols:(dx + 1) * d.cols] = grad.astype(bf16)

        if rolled:
            pl.loop(0, 2)(lambda r: rows_step(pl.ds(pl.multiple_of(r * half, half), half)))
        else:
            for r in range(2):
                rows_step(slice(r * half, (r + 1) * half))
        for dx in range(2):
            copy = pltpu.make_async_copy(
                buf.at[i, dx], act.at[:, pl.ds(cols[dx], d.cols)], sem.at[i, dx])
            copy.start()
            copies.append(copy)
    for copy in copies:
        copy.wait()


def forward(d, steps, xs, cot, ws, act=None, rolled=False):
    slots = len(steps)
    ops = Operands()
    ops.add(cot)
    need = {source(g, t) for _, g in steps for t in range(d.taps)}
    xs = {k: (ops.add(a), blk) for k, (a, blk) in xs.items() if k in need}
    shards = {}
    for dy, g in steps:
        for dx in range(2):
            shards.setdefault((dy, dx), {}).update(ops.shard(ws[dy, dx], d, g))
    operands = list(ops.arrays)
    count = len(operands)
    specs = [vspec()] * count
    aliases = {}
    if act is not None:
        aliases = {count: 0}
        operands.append(act)
        specs.append(pl.BlockSpec(memory_space=pl.ANY))
    out = call(
        functools.partial(forward_body, d, steps, shards, count, xs, act is not None, rolled),
        operands,
        [jax.ShapeDtypeStruct((d.n, d.width), bf16),
         jax.ShapeDtypeStruct((slots, d.n, 2 * d.cols), bf16)],
        22, 2 * d.n * d.taps * d.blk * 2 * d.cols * slots, 8 * d.n * d.cols * slots,
        specs=specs, out_specs=[pl.BlockSpec(memory_space=pl.ANY), vspec()],
        scratch=[pltpu.VMEM((slots, 2, d.n, d.cols), bf16), pltpu.SemaphoreType.DMA((slots, 2))],
        aliases=aliases)
    return out[0], {step: (out[1], i) for i, step in enumerate(steps)}


def wgrad_body(d, steps, where, count, xts, gps, copied, *refs):
    ops, outs = refs[:count], refs[count:]
    part = d.blk // 2
    for out, row, ref, rows in copied:
        outs[out][row * d.blk:(row + rows) * d.blk, :] = ops[ref][...]
    for dy, g in steps:
        ref, at = gps[dy, g]
        gp = ops[ref][at]

        @pl.loop(0, 2)
        def _(r):
            for t in range(d.taps):
                ref, blk = xts[source(g, t)]
                rows = pl.ds(pl.multiple_of(blk * d.blk + r * part, part), part)
                v = jnp.dot(ops[ref][rows, :], gp, preferred_element_type=f32)
                for dx in range(2):
                    out, row = where[dy, dx][g * d.taps + t]
                    rows = pl.ds(pl.multiple_of(row * d.blk + r * part, part), part)
                    outs[out][rows, :] = v[:, dx * d.cols:(dx + 1) * d.cols].astype(outs[out].dtype)


def wgrad(d, steps, xts, gps, pieces, carried=None):
    ops = Operands()
    where = {(dy, dx): {} for dy, _ in steps for dx in range(2)}
    shapes, copied = [], []
    for i, piece in enumerate(pieces):
        row = 0
        if carried and i in carried:
            row = carried[i].shape[0] // d.blk
            copied.append((i, 0, ops.add(carried[i]), row))
        for owner, tiles in piece:
            for tile in tiles:
                where[owner][tile] = (i, row)
                row += 1
        kind = f32 if owner == (0, 0) else bf16
        shapes.append(jax.ShapeDtypeStruct((row * d.blk, d.cols), kind))
    need = {source(g, t) for _, g in steps for t in range(d.taps)}
    xts = {k: (ops.add(a), blk) for k, (a, blk) in xts.items() if k in need}
    gps = {step: (ops.add(gps[step][0]), gps[step][1]) for step in steps}
    count = len(ops.arrays)
    return call(functools.partial(wgrad_body, d, steps, where, count, xts, gps, copied),
                ops.arrays, shapes, 20,
                4 * d.n * d.taps * d.blk * d.cols * len(steps), 2 * d.n * d.n * len(steps))


def dgrad_body(d, outs_of, shards, count, gps, *refs):
    ops, outs = refs[:count], refs[count:]
    half = d.n // 2
    for out, jobs in zip(outs, outs_of):
        for lane, products in enumerate(jobs):
            w = jnp.concatenate([tile_of(d, ops, shards[dy, dx], g, t) for t, g in products
                                 for dy in range(4) for dx in range(2)], axis=1)
            for r in range(2):
                rows = slice(r * half, (r + 1) * half)
                gp = jnp.concatenate([ops[gps[dy, g][0]][gps[dy, g][1], rows, :]
                                      for _, g in products for dy in range(4)], axis=1)
                v = lax.dot_general(gp, w, (((1,), (1,)), ((), ())), preferred_element_type=f32)
                out[rows, lane * d.blk:(lane + 1) * d.blk] = v.astype(out.dtype)


def dgrad(d, outs, gps, ws):
    ops = Operands()
    groups = sorted({g for o in outs for job in o for _, g in job})
    gps = {(dy, g): (ops.add(gps[dy, g][0]), gps[dy, g][1]) for dy in range(4) for g in groups}
    shards = {o: {} for o in ws}
    for o in ws:
        for g in groups:
            shards[o].update(ops.shard(ws[o], d, g))
    count = len(ops.arrays)
    jobs = sum(len(j) for o in outs for j in o)
    shapes = [jax.ShapeDtypeStruct((d.n, d.blk * len(o)), f32 if len(o[0]) > 1 else bf16)
              for o in outs]
    return call(functools.partial(dgrad_body, d, outs, shards, count, gps), ops.arrays, shapes,
                20, 16 * d.n * jobs * d.blk * d.cols, d.n * d.n * jobs)


def transpose_body(*refs):
    k = len(refs) // 2
    for a, b in zip(refs[:k], refs[k:]):
        b[...] = a[...].T


def transposed(xs):
    return call(transpose_body, xs,
                [jax.ShapeDtypeStruct(x.shape[::-1], x.dtype) for x in xs], 12, 0, 1 << 20)


def combine_body(plan, count, scale, *refs):
    outs = refs[count:]
    step = 256
    for out, pieces in zip(outs, plan):
        for lo, hi, terms in pieces:
            @pl.loop(0, (hi - lo) // step)
            def _(i):
                total = None
                for ref, row in terms:
                    term = refs[ref][pl.ds(pl.multiple_of(row + i * step, step), step), :]
                    if len(terms) > 1:
                        term = term.astype(f32)
                    total = term if total is None else total + term
                if scale is not None:
                    total = total * scale
                out[pl.ds(pl.multiple_of(lo + i * step, step), step), :] = total.astype(out.dtype)


def combine(outs, dtype=bf16, scale=None):
    ops = Operands()
    plan, shapes = [], []
    for pieces in outs:
        lo, entry = 0, []
        for rows, terms in pieces:
            entry.append((lo, lo + rows, [(ops.add(a), r) for a, r in terms]))
            lo += rows
        plan.append(entry)
        shapes.append(jax.ShapeDtypeStruct((lo, pieces[0][1][0][0].shape[1]), dtype))
    return call(functools.partial(combine_body, plan, len(ops.arrays), scale), ops.arrays,
                shapes, 16, 0, 1 << 20)


def grad_input_body(d, count, *refs):
    whole, halves, out = refs[:count], refs[count:-1], refs[-1]
    per = len(halves) // d.groups
    step = 128

    @pl.loop(0, d.n // step)
    def _(i):
        rows = pl.ds(pl.multiple_of(i * step, step), step)
        for g in range(d.groups):
            lanes = slice(g * d.blk, (g + 1) * d.blk)
            total = whole[0][rows, lanes]
            for ref in whole[1:]:
                total = total + ref[rows, lanes].astype(f32)
            for ref in halves[g * per:(g + 1) * per]:
                total = total + ref[rows, :].astype(f32)
            out[rows, lanes] = total.astype(out.dtype)


def grad_input(d, here, whole, halves):
    return call(functools.partial(grad_input_body, d, 1 + len(whole)),
                [here, *whole, *halves[0], *halves[1]],
                [jax.ShapeDtypeStruct((d.n, d.groups * d.blk), bf16)], 16, 0, 1 << 20)[0]


def step(features, weight, cotangent):
    d = Dims(features, weight)
    w = weight.reshape(d.tiles * d.blk, d.cols)
    t_a, t_l, t_h = range(0, 10), range(0, 5), range(5, 10)
    t_b, t_0, t_1, t_all = range(10, 14), range(0, 7), range(7, 14), range(14)
    h_0, h_1 = range(5, 7), range(7, 10)
    A, L, B, G = 10 * d.blk, 5 * d.blk, 4 * d.blk, 7 * d.blk

    u, m = up(w), down(w)
    wa, wb = combine([[(A, [(w, 0)])], [(B, [(w, A)])]])
    sa = side(wa)
    su, sm = up(sa), down(sa)
    ulo, mhi, ub = combine([[(G, [(u, 0)])], [(G, [(m, G)])],
                            [(B, [(u, A)]), (B, [(m, A)]), (B, [(wb, 0)])]])
    fl, fh, ub = up(ulo), down(mhi), side(ub)
    slo, shi = combine([[(L, [(su, 0)])], [(L, [(sm, L)])]])
    gl, gh = up(slo), down(shi)
    gb = side(combine([[(B, [(fh, A - G)])]])[0])
    ws = {
        (0, 0): Tiles((w, 0, t_all)),
        (3, 0): Tiles((u, 0, t_all)),
        (1, 0): Tiles((m, 0, t_all)),
        (2, 0): Tiles((fl, 0, t_0), (fh, 0, t_1)),
        (0, 1): Tiles((sa, 0, t_a), (ub, 8, t_b)),
        (3, 1): Tiles((su, 0, t_a), (ub, 0, t_b)),
        (1, 1): Tiles((sm, 0, t_a), (ub, 4, t_b)),
        (2, 1): Tiles((gl, 0, t_l), (gh, 0, t_h), (gb, 0, t_b)),
    }

    fa, fb = features[:, :d.blk], features[:, d.blk:]
    x1 = flip(features, "c", 1)
    x2 = [flip(fa, "z", 1), flip(fb, "z", 1)]
    x3 = [flip(fa, "z", 2), flip(fb, "z", 2)]
    x4 = [flip(x3[0], "z", 6), flip(x3[1], "z", 6)]
    x5 = flip(features, "xh", 1)
    keys = [(src, blk) for src in range(6) for blk in range(2)]

    def placed(whole, split):
        it = {0: whole[0], 1: whole[1], 5: whole[2]}
        return {(src, blk): (it[src], blk) if src in it else (split[src - 2][blk], 0)
                for src, blk in keys}

    xs = placed([features, x1, x5], [x2, x3, x4])
    *t_whole, t2a, t3a, t4a = transposed([features, x1, x5, x2[0], x3[0], x4[0]])
    t2b, t3b, t4b = transposed([x2[1], x3[1], x4[1]])
    xts = placed(t_whole, [[t2a, t2b], [t3a, t3b], [t4a, t4b]])

    gps = {}
    act, more = forward(d, [(0, 0)], xs, cotangent, ws, rolled=True)
    gps.update(more)

    def run(steps, rolled=False):
        nonlocal act
        act, more = forward(d, steps, xs, cotangent, ws, act, rolled)
        gps.update(more)

    run([(1, 0), (3, 0)])
    pd, pul, pu0, hu, hd = wgrad(d, [(1, 0), (3, 0)], xts, gps, [
        [((1, 1), t_l), ((1, 0), t_0)], [((3, 1), t_l)], [((3, 0), t_0)],
        [((3, 1), h_0)], [((1, 1), h_0)]])
    r1 = up(pd)
    run([(2, 0)])
    pfl, pf0, hf = wgrad(d, [(2, 0)], xts, gps, [
        [((2, 1), t_l)], [((2, 0), t_0)], [((2, 1), h_0)]])
    el, rfl = down(pfl), down(pf0)
    p5a, p4a = dgrad(d, [[[(5, 0)]], [[(4, 0)]]], gps, ws)
    z5a = flip(p5a, "z", 6)
    p4a, = combine([[(d.n, [(p4a, 0), (z5a, 0)])]])
    z4a = flip(p4a, "z", 2)
    run([(2, 1)])
    pfh, pfb, pf1 = wgrad(d, [(2, 1)], xts, gps, [
        [((2, 1), h_1)], [((2, 1), t_b)], [((2, 0), t_1)]], {0: hf})
    eh, eb = up(pfh), side(pfb)
    run([(1, 1), (3, 1)])
    puh, pdh, pub, pu1, pd1 = wgrad(d, [(1, 1), (3, 1)], xts, gps, [
        [((3, 1), h_1)], [((1, 1), h_1)], [((3, 1), t_b), ((1, 1), t_b)],
        [((3, 0), t_1)], [((1, 0), t_1)]], {0: hu, 1: hd})
    rub = side(pub)
    run([(0, 1)], True)
    p5b, p6, p4b, p3 = dgrad(d, [[[(5, 1)]], [[(6, 0)], [(6, 1)]], [[(4, 1)]],
                                 [[(3, 0)], [(3, 1)]]], gps, ws)
    z5b, z3 = flip(p5b, "z", 6), flip(p3, "z", 1)
    p4b, = combine([[(d.n, [(p4b, 0), (z5b, 0)])]])
    z4b = flip(p4b, "z", 2)

    pu, = combine([[(L, [(pul, 0), (el, 0)]), (L, [(puh, 0)])]])
    ru = down(pu)
    rd, = combine([[(L, [(pdh, 0), (eh, 0)]),
                    (A - G, [(pf1, 0)]), (B, [(pf1, A - G), (eb, 0)])]])
    rd = up(rd)
    p2, here = dgrad(d, [
        [[(2, 0)], [(2, 1)]], [[(0, 0), (1, 1)], [(0, 1), (1, 0)]]], gps, ws)
    zx, zc = flip(p6, "xh", 1), flip(p2, "c", 1)
    pu, = combine([[(G, [(pu0, 0), (rfl, 0)]), (A - G, [(pu1, 0)]),
                    (B, [(pu1, A - G), (rub, 0)])]])
    q0 = down(pu)
    mine, psa, psb = wgrad(d, [(0, 0), (0, 1)], xts, gps, [
        [((0, 0), t_all)], [((0, 1), t_a)], [((0, 1), t_b)]])
    q2b = side(psb)
    psa, = combine([[(L, [(psa, 0), (ru, 0), (r1, 0)]), (L, [(psa, L), (ru, L), (rd, 0)])]])
    q2a = side(psa)
    pd1, = combine([[(A - G, [(pd1, 0), (rd, L)]),
                     (B, [(pd1, A - G), (rd, L + A - G), (rub, B)])]])
    q1h = up(pd1)
    gx = grad_input(d, here, [zc, z3, zx], [[z4a], [z4b]])
    gw, = combine([[
        (G, [(mine, 0), (q0, 0), (r1, L), (q2a, 0)]),
        (A - G, [(mine, G), (q0, G), (q1h, 0), (q2a, G)]),
        (B, [(mine, A), (q0, A), (q1h, A - G), (q2b, 0)])]],
        f32, float(d.n * 8) ** (-0.5))
    return (act, gx, gw.reshape(weight.shape))


def solution(mesh):
    torus = Mesh(mesh.devices.reshape(4, 2, 2, 8, 2), ("y", "xl", "xh", "z", "c"))
    dp, feat = ("y", "xl"), ("xh", "z", "c")
    placed = (P(dp, feat), P(feat, None, None, dp), P(dp, feat))
    return jax.shard_map(
        step,
        mesh=torus,
        in_specs=placed,
        out_specs=(P(dp, feat), P(dp, feat), P(feat, None, None, dp)),
        check_vma=False,
    )
```
